512 devices in a mesh: row: 64 (over z, y), col: 8 (over x, core).
Axes of the slice: x: 4, y: 4, z: 16, core: 2. Of those that a mesh axis runs over, the one named last changes fastest.
Arguments:
- amplitudes: bfloat16 [2048, 16384], P('row', 'col'), may hold values from -6 to 6
- integrals: bfloat16 [2048, 16384], P('col', 'row'), may hold values from -0.125 to 0.125
- amp_mask: int32 [64, 128], replicated, may hold values 0 or 1
- int_mask: int32 [64, 128], replicated, may hold values 0 or 1
Outputs:
- scaled_residual: float32 [16384, 16384], P('col', 'row')
- row_norm: float32 [16384], P('col')
The draws below stay inside these ranges and needn't reach their ends.
Inputs may be any that keep to these rules, and one draw needn't show every extreme that they name: `amp_mask`: an entry of 1 keeps its tile, 0 drops it. `int_mask`: an entry of 1 keeps its tile, 0 drops it.
All inputs are finite; a program needn't handle non-finite values.
Results may differ from the reference program's by a relative error of at most 0.0003.
Values may be sent and summed in bfloat16 or wider, within the bound.
A program may use at most 64 MiB of HBM per device.

```python
import jax
import jax.numpy as jnp
from jax import lax

OCC = 128
TILE = 128
KB = 32
M = 16384
K = 2048
NPAIR = 16384


def with_ends(entries, key, low, top_value):
    longest = entries.shape.index(max(entries.shape))
    spots = []
    for shift in (0, 1):
        where = [jax.random.randint(jax.random.fold_in(key, axis), (), 0, length) for axis, length in enumerate(entries.shape)]
        where[longest] = (where[longest] + shift) % entries.shape[longest]
        spots.append(tuple(where))
    return entries.at[spots[0]].set(low).at[spots[1]].set(top_value)


def levels(key, dims, split, smallest, largest):
    gain = 1.0
    for position, blocks in split:
        draws = jax.random.uniform(jax.random.fold_in(jax.random.fold_in(key, 6), position), (blocks,), jnp.float32, smallest / len(split), largest / len(split))
        gain = gain * jnp.repeat(jnp.exp(draws), dims[position] // blocks).reshape((-1,) + (1,) * (len(dims) - 1 - position))
    return gain


def scatter_about(rng, dims, deviation, most, cuts=(), dtype=jnp.bfloat16):
    result = deviation * jax.random.normal(rng, dims, jnp.float32)
    if cuts:
        result = result * levels(rng, dims, cuts, -0.22, 0.18)
    return jnp.clip(result, -most, most).astype(dtype)


def setup_inputs(seed: int = 0) -> dict:
    arg_keys = jax.random.split(jax.random.key(seed), 5)
    amplitudes = scatter_about(arg_keys[0], (K, M), 1.0, 6.0, ((0, 64), (1, 8)))
    integrals = scatter_about(arg_keys[1], (K, NPAIR), K ** -0.5, 0.125, ((0, 8), (1, 64)))
    amp_mask = with_ends((jax.random.randint(arg_keys[2], (K // KB, M // TILE), 0, 2) < 1).astype(jnp.int32), jax.random.fold_in(arg_keys[2], 1), 0, 1)
    int_mask = with_ends((jax.random.randint(arg_keys[3], (K // KB, NPAIR // TILE), 0, 2) < 1).astype(jnp.int32), jax.random.fold_in(arg_keys[3], 1), 0, 1)
    return {"amplitudes": amplitudes, "integrals": integrals, "amp_mask": amp_mask, "int_mask": int_mask}


def expand(keep, rows, cols):
    return jnp.repeat(jnp.repeat(keep, rows, axis=0), cols, axis=1).astype(jnp.bfloat16)

def reference(amplitudes, integrals, amp_mask, int_mask):
    masked_amp = amplitudes * expand(amp_mask, KB, TILE)
    masked_int = integrals * expand(int_mask, KB, TILE)
    ladder = lax.dot_general(masked_amp, masked_int, (((0,), (0,)), ((), ())), preferred_element_type=jnp.float32)
    width = ladder.shape[1]
    mirror = ladder.reshape(OCC, OCC, width).transpose(1, 0, 2).reshape(OCC * OCC, width)
    summed = ladder + mirror
    row_norm = jnp.sqrt(lax.optimization_barrier(jnp.sum(summed * summed, axis=1)) / width + 1e-06)
    return (summed / row_norm[:, None], row_norm)
```

```python
import functools

import jax
import jax.numpy as jnp
from jax import lax
from jax.experimental import pallas as pl
from jax.experimental.pallas import tpu as pltpu
from jax.sharding import PartitionSpec as P

TILE = 128
OCC = 128
Y = 4
H = 2
MESH = pl.DeviceIdType.MESH
WIDTH = 16384


def kernel(
    nz, nc, am_ref, bm_ref, a_ref, b_ref, s_ref, n_ref,
    A, B, L, R, NZ, NY,
    loc_sem,
    pz_s, pz_r, qz_s, qz_r, py_s, py_r, qy_s, qy_r,
    b_s, b_r, x_s, x_r, nz_s, nz_r, ny_s, ny_r,
):
    kb, m_dev = a_ref.shape
    kc, n_dev = b_ref.shape
    mh = m_dev // H
    cp = (mh * 5 // 8) // TILE * TILE
    half = kb // 2
    bun = Y * kb
    occ = m_dev // OCC
    oh = occ // H
    far = nz // 2
    r = lax.axis_index("row")
    c = lax.axis_index("col")
    z = r // Y
    y = r % Y

    def at_z(d):
        return (lax.rem(z + d + 2 * nz, nz) * Y + y, c)

    def at_y(d):
        return (z * Y + lax.rem(y + d + 2 * Y, Y), c)

    def at_c(k):
        return (r, lax.rem(c + k, nc))

    def remote(src, dst, ss, rs, dev):
        return pltpu.make_async_remote_copy(
            src_ref=src, dst_ref=dst, send_sem=ss, recv_sem=rs,
            device_id=dev, device_id_type=MESH,
        )

    for t in range(m_dev // TILE):
        keep = am_ref[r, c * (m_dev // TILE) + t].astype(jnp.float32)
        lo = t * TILE
        val = (a_ref[:, lo:lo + TILE].astype(jnp.float32) * keep).astype(jnp.bfloat16)
        A[lo // mh, pl.ds(pl.multiple_of(r * kb, kb), kb), lo % mh:lo % mh + TILE] = val
    for u in range(kc // kb):
        for t in range(n_dev // TILE):
            keep = bm_ref[c * (kc // kb) + u, r * (n_dev // TILE) + t].astype(jnp.float32)
            val = b_ref[u * kb:(u + 1) * kb, t * TILE:(t + 1) * TILE].astype(jnp.float32) * keep
            B[pl.ds(pl.multiple_of(c * kc + u * kb, kb), kb), t * TILE:(t + 1) * TILE] = val.astype(jnp.bfloat16)

    barrier = pltpu.get_barrier_semaphore()
    for k in range(1, nz):
        pl.semaphore_signal(barrier, inc=1, device_id=at_z(k), device_id_type=MESH)
    for k in range(1, Y):
        pl.semaphore_signal(barrier, inc=1, device_id=at_y(k), device_id_type=MESH)
    for k in range(1, nc):
        pl.semaphore_signal(barrier, inc=1, device_id=at_c(k), device_id_type=MESH)
    pl.semaphore_wait(barrier, nz - 1 + Y - 1 + nc - 1)

    def block(h, dz, dy, first, rows):
        zz = lax.rem(z + dz + 2 * nz, nz)
        yy = lax.rem(y + dy + 2 * Y, Y)
        return A.at[h, pl.ds(pl.multiple_of((zz * Y + yy) * kb + first, half), rows), :cp]

    def bundle(h, dz, first, rows):
        zz = lax.rem(z + dz + 2 * nz, nz)
        return A.at[h, pl.ds(pl.multiple_of(zz * bun + first, half), rows), cp:]

    sign = (1, -1)

    def pz(h, d, s, back, last):
        ref = block(h, -sign[d] * (s - 1 + back), 0, d * half if last else 0, half if last else kb)
        return remote(ref, ref, pz_s.at[h, d, s], pz_r.at[h, d, s], at_z(sign[d]))

    def qz(h, d, s, back, last):
        ref = bundle(h, -sign[d] * (s - 1 + back), d * (bun // 2) if last else 0, bun // 2 if last else bun)
        return remote(ref, ref, qz_s.at[h, d, s], qz_r.at[h, d, s], at_z(sign[d]))

    def py(h, slot, dz, kind, back):
        d = kind % 2
        whole = kind < 2
        dy = -sign[d] * ((0 if whole else 1) + back)
        ref = block(h, dz, dy, 0 if whole else d * half, kb if whole else half)
        return remote(ref, ref, py_s.at[h, slot, kind], py_r.at[h, slot, kind], at_y(sign[d]))

    def qy(h, k, back):
        yy = lax.rem(y - back * k + 2 * Y, Y)
        ref = A.at[h, pl.ds(pl.multiple_of((z * Y + yy) * kb, kb), kb), cp:]
        return remote(ref, ref, qy_s.at[h, k], qy_r.at[h, k], at_y(k))

    def slot_of(d, s):
        return s if d == 0 else far + s

    def spread(h, slot, dz):
        py(h, slot, dz, 0, 0).start()
        py(h, slot, dz, 1, 0).start()

    def relay(h, slot, dz):
        py(h, slot, dz, 0, 1).wait_recv()
        py(h, slot, dz, 2, 0).start()
        py(h, slot, dz, 1, 1).wait_recv()
        py(h, slot, dz, 3, 0).start()

    def begin(h):
        for k in (1, 3, 2):
            qy(h, k, 0).start()
        for d in range(2):
            pz(h, d, 1, 0, False).start()
        spread(h, 0, 0)

    def step(h, s, first=False, last=False):
        for d in range(2):
            pz(h, d, s, 1, False).wait_recv()
            pz(h, d, s + 1, 0, last).start()
            spread(h, slot_of(d, s), -sign[d] * s)
        if first:
            relay(h, 0, 0)
        else:
            for d in range(2):
                relay(h, slot_of(d, s - 1), -sign[d] * (s - 1))
        for d in range(2):
            qz(h, d, s, 1, False).wait_recv()
            qz(h, d, s + 1, 0, last).start()

    def gather(h):
        for k in (1, 3, 2):
            qy(h, k, 1).wait_recv()
        for d in range(2):
            qz(h, d, 1, 0, False).start()
        step(h, 1, first=True)

        def body(s, carry):
            step(h, s)
            return carry

        lax.fori_loop(2, far - 1, body, 0)
        step(h, far - 1, last=True)
        for d in range(2):
            pz(h, d, far, 1, True).wait_recv()
        spread(h, far, far)
        for d in range(2):
            relay(h, slot_of(d, far - 1), -sign[d] * (far - 1))
        if h + 1 < H:
            begin(h + 1)
        for d in range(2):
            qz(h, d, far, 1, True).wait_recv()
        relay(h, far, far)

        def rest(i, carry):
            dz = jnp.where(i <= far, -i, i - far)
            for kind in (2, 3):
                py(h, i, dz, kind, 1).wait_recv()
            return carry

        lax.fori_loop(0, nz, rest, 0)

    def b_copy(k, back):
        src = lax.rem(c - back * k + nc, nc)
        ref = B.at[pl.ds(pl.multiple_of(src * kc, kc), kc), :]
        return remote(ref, ref, b_s.at[k], b_r.at[k], at_c(k))

    def x_copy(h, k, back):
        to = lax.rem(c + (1 - back) * k, nc)
        src = lax.rem(c - back * k + nc, nc)
        return remote(
            L.at[pl.ds(h * oh, oh), pl.ds(pl.multiple_of(to * occ, occ), occ), :],
            R.at[src, pl.ds(h * oh, oh)],
            x_s.at[h, k], x_r.at[h, k], at_c(k),
        )

    def n_copy(buf, ss, rs, me, k, n, dev, back):
        ref = buf.at[lax.rem(me - back * k + n, n)]
        return remote(ref, ref, ss.at[k], rs.at[k], dev)

    begin(0)
    for k in range(1, nc):
        b_copy(k, 0).start()
    for h in range(H):
        gather(h)
        if h == 0:
            for k in range(1, nc):
                b_copy(k, 1).wait_recv()

        def product(i, carry):
            cols = pl.ds(pl.multiple_of(i * 2 * OCC, 2 * OCC), 2 * OCC)
            part = lax.dot_general(
                A[h, :, cols], B[...], (((0,), (0,)), ((), ())), preferred_element_type=jnp.float32
            )
            L[pl.ds(h * oh + 2 * i, 2)] = part.reshape(2, OCC, n_dev)
            return carry

        lax.fori_loop(0, oh // 2, product, 0)
        for k in range(1, nc):
            x_copy(h, k, 0).start()
        own = pltpu.make_async_copy(
            L.at[pl.ds(h * oh, oh), pl.ds(pl.multiple_of(c * occ, occ), occ), :],
            R.at[c, pl.ds(h * oh, oh)],
            loc_sem.at[h],
        )
        own.start()
        own.wait()

    for h in range(H):
        for k in range(1, nc):
            x_copy(h, k, 1).wait_recv()

        def add(src, carry):
            for o in range(0, oh, 8):
                got = jnp.swapaxes(R[src, pl.ds(h * oh + o, 8)], 0, 1)
                at = pl.ds(pl.multiple_of(src * occ + h * oh + o, 8), 8)
                s_ref[:, at, :] = L[:, at, :] + got
            return carry

        lax.fori_loop(0, nc, add, 0)

    def squares(i, carry):
        v = s_ref[i]
        v = v * v
        t = v[:, :TILE]
        for q in range(1, n_dev // TILE):
            t = t + v[:, q * TILE:(q + 1) * TILE]
        NZ[z, pl.ds(i, 1), :] = jnp.sum(t.T, axis=0, keepdims=True)
        return carry

    lax.fori_loop(0, occ, squares, 0)
    for k in range(1, nz):
        n_copy(NZ, nz_s, nz_r, z, k, nz, at_z(k), 0).start()
    for k in range(1, nz):
        n_copy(NZ, nz_s, nz_r, z, k, nz, at_z(k), 1).wait_recv()
    total = NZ[0]
    for q in range(1, nz):
        total = total + NZ[q]
    NY[y] = total
    for k in range(1, Y):
        n_copy(NY, ny_s, ny_r, y, k, Y, at_y(k), 0).start()
    for k in range(1, Y):
        n_copy(NY, ny_s, ny_r, y, k, Y, at_y(k), 1).wait_recv()
    total = NY[0]
    for q in range(1, Y):
        total = total + NY[q]
    n_ref[...] = jnp.sqrt(total / WIDTH + 1e-06)

    for h in range(H):
        for d in range(2):
            def sent(s, carry):
                pz(h, d, s, 0, False).wait_send()
                qz(h, d, s, 0, False).wait_send()
                return carry

            lax.fori_loop(1, far, sent, 0)
            pz(h, d, far, 0, True).wait_send()
            qz(h, d, far, 0, True).wait_send()

        def sent_y(i, carry):
            dz = jnp.where(i <= far, -i, i - far)
            for kind in range(4):
                py(h, i, dz, kind, 0).wait_send()
            return carry

        lax.fori_loop(0, nz, sent_y, 0)
        for k in range(1, Y):
            qy(h, k, 0).wait_send()
        for k in range(1, nc):
            x_copy(h, k, 0).wait_send()
    for k in range(1, nc):
        b_copy(k, 0).wait_send()
    for k in range(1, nz):
        n_copy(NZ, nz_s, nz_r, z, k, nz, at_z(k), 0).wait_send()
    for k in range(1, Y):
        n_copy(NY, ny_s, ny_r, y, k, Y, at_y(k), 0).wait_send()


def local(nrow, nc, amplitudes, integrals, amp_mask, int_mask):
    kb, m_dev = amplitudes.shape
    kc, n_dev = integrals.shape
    nz = nrow // Y
    k_all = kb * nrow
    occ = m_dev // OCC
    far = nz // 2
    dma = pltpu.SemaphoreType.DMA
    pairs = [(H, 2, far + 1), (H, 2, far + 1), (H, nz, 4), (H, Y), (nc,), (H, nc), (nz,), (Y,)]
    summed, norm = pl.pallas_call(
        functools.partial(kernel, nz, nc),
        out_shape=(
            jax.ShapeDtypeStruct((occ, OCC, n_dev), jnp.float32),
            jax.ShapeDtypeStruct((occ, OCC), jnp.float32),
        ),
        in_specs=[
            pl.BlockSpec(memory_space=pltpu.SMEM),
            pl.BlockSpec(memory_space=pltpu.SMEM),
            pl.BlockSpec(memory_space=pltpu.VMEM),
            pl.BlockSpec(memory_space=pltpu.VMEM),
        ],
        out_specs=(
            pl.BlockSpec(memory_space=pltpu.VMEM),
            pl.BlockSpec(memory_space=pltpu.VMEM),
        ),
        scratch_shapes=[
            pltpu.VMEM((H, k_all, m_dev // H), jnp.bfloat16),
            pltpu.VMEM((k_all, n_dev), jnp.bfloat16),
            pltpu.VMEM((occ, OCC, n_dev), jnp.float32),
            pltpu.VMEM((nc, occ, occ, n_dev), jnp.float32),
            pltpu.VMEM((nz, occ, OCC), jnp.float32),
            pltpu.VMEM((Y, occ, OCC), jnp.float32),
            dma((H,)),
        ] + [dma(p) for p in pairs for _ in range(2)],
        compiler_params=pltpu.CompilerParams(
            collective_id=0, has_side_effects=True, vmem_limit_bytes=40 << 20,
        ),
    )(amp_mask, int_mask, amplitudes, integrals)
    return summed.reshape(m_dev, n_dev) / norm.reshape(m_dev)[:, None], norm.reshape(m_dev)


def solution(mesh):
    return jax.shard_map(
        functools.partial(local, mesh.shape["row"], mesh.shape["col"]),
        mesh=mesh,
        in_specs=(P("row", "col"), P("col", "row"), P(), P()),
        out_specs=(P("col", "row"), P("col")),
        check_vma=False,
    )
```

```python
import functools

import jax
import jax.numpy as jnp
from jax import lax
from jax.experimental import pallas as pl
from jax.experimental.pallas import tpu as pltpu
from jax.sharding import PartitionSpec as P

TILE = 128
OCC = 128
Y = 4
H = 2
MESH = pl.DeviceIdType.MESH
WIDTH = 16384


def kernel(
    nz, nc, am_ref, bm_ref, a_ref, b_ref, s_ref, n_ref,
    A, B, L, R, NZ, NY,
    a_own, b_own, am_own, bm_own, in_sem,
    loc_sem,
    pz_s, pz_r, qz_s, qz_r, py_s, py_r, qy_s, qy_r,
    b_s, b_r, x_s, x_r, nz_s, nz_r, ny_s, ny_r,
):
    kb, m_dev = a_ref.shape
    kc, n_dev = b_ref.shape
    mh = m_dev // H
    cp = (mh * 5 // 8) // TILE * TILE
    half = kb // 2
    occ = m_dev // OCC
    oh = occ // H
    far = nz // 2
    r = lax.axis_index("row")
    c = lax.axis_index("col")
    z = r // Y
    y = r % Y

    def at_z(d):
        return (lax.rem(z + d + 2 * nz, nz) * Y + y, c)

    def at_y(d):
        return (z * Y + lax.rem(y + d + 2 * Y, Y), c)

    def at_c(k):
        return (r, lax.rem(c + k, nc))

    def remote(src, dst, ss, rs, dev):
        return pltpu.make_async_remote_copy(
            src_ref=src, dst_ref=dst, send_sem=ss, recv_sem=rs,
            device_id=dev, device_id_type=MESH,
        )

    loads = (
        pltpu.make_async_copy(am_ref.at[pl.ds(pl.multiple_of(r // 8 * 8, 8), 8)], am_own, in_sem.at[0]),
        pltpu.make_async_copy(bm_ref.at[pl.ds(pl.multiple_of(c * (kc // kb), kc // kb), kc // kb)], bm_own, in_sem.at[1]),
        pltpu.make_async_copy(a_ref, a_own, in_sem.at[2]),
        pltpu.make_async_copy(b_ref, b_own, in_sem.at[3]),
    )
    for load in loads:
        load.start()

    barrier = pltpu.get_barrier_semaphore()
    for k in range(1, nz):
        pl.semaphore_signal(barrier, inc=1, device_id=at_z(k), device_id_type=MESH)
    for k in range(1, Y):
        pl.semaphore_signal(barrier, inc=1, device_id=at_y(k), device_id_type=MESH)
    for k in range(1, nc):
        pl.semaphore_signal(barrier, inc=1, device_id=at_c(k), device_id_type=MESH)

    for load in loads:
        load.wait()
    for t in range(m_dev // TILE):
        keep = am_own[r % 8, c * (m_dev // TILE) + t].astype(jnp.float32)
        lo = t * TILE
        val = (a_own[:, lo:lo + TILE].astype(jnp.float32) * keep).astype(jnp.bfloat16)
        A[lo // mh, pl.ds(pl.multiple_of(r * kb, kb), kb), lo % mh:lo % mh + TILE] = val
    for u in range(kc // kb):
        for t in range(n_dev // TILE):
            keep = bm_own[u, r * (n_dev // TILE) + t].astype(jnp.float32)
            val = b_own[u * kb:(u + 1) * kb, t * TILE:(t + 1) * TILE].astype(jnp.float32) * keep
            B[pl.ds(pl.multiple_of(c * kc + u * kb, kb), kb), t * TILE:(t + 1) * TILE] = val.astype(jnp.bfloat16)
    pl.semaphore_wait(barrier, nz - 1 + Y - 1 + nc - 1)

    def block(h, dz, dy, first, rows):
        zz = lax.rem(z + dz + 2 * nz, nz)
        yy = lax.rem(y + dy + 2 * Y, Y)
        return A.at[h, pl.ds(pl.multiple_of((zz * Y + yy) * kb + first, half), rows), :cp]

    def rest_of(h, dz, dy, first, rows):
        zz = lax.rem(z + dz + 2 * nz, nz)
        yy = lax.rem(y + dy + 2 * Y, Y)
        return A.at[h, pl.ds(pl.multiple_of((zz * Y + yy) * kb + first, half), rows), cp:]

    sign = (1, -1)

    def pz(h, d, s, back, last):
        ref = block(h, -sign[d] * (s - 1 + back), 0, d * half if last else 0, half if last else kb)
        return remote(ref, ref, pz_s.at[h, d, s], pz_r.at[h, d, s], at_z(sign[d]))

    def qz(h, d, s, e, back, last):
        ref = rest_of(h, -sign[d] * (s - 1 + back), e, d * half if last else 0, half if last else kb)
        return remote(ref, ref, qz_s.at[h, d, s, e], qz_r.at[h, d, s, e], at_z(sign[d]))

    def py(h, slot, dz, kind, back):
        d = kind % 2
        whole = kind < 2
        dy = -sign[d] * ((0 if whole else 1) + back)
        ref = block(h, dz, dy, 0 if whole else d * half, kb if whole else half)
        return remote(ref, ref, py_s.at[h, slot, kind], py_r.at[h, slot, kind], at_y(sign[d]))

    def qy(h, k, back):
        ref = rest_of(h, 0, -back * k, 0, kb)
        return remote(ref, ref, qy_s.at[h, k], qy_r.at[h, k], at_y(k))

    def slot_of(d, s):
        return s if d == 0 else far + s

    def spread(h, slot, dz):
        py(h, slot, dz, 0, 0).start()
        py(h, slot, dz, 1, 0).start()

    def relay(h, slot, dz):
        py(h, slot, dz, 0, 1).wait_recv()
        py(h, slot, dz, 2, 0).start()
        py(h, slot, dz, 1, 1).wait_recv()
        py(h, slot, dz, 3, 0).start()

    order = (0, 3, 1, 2)

    def begin(h):
        for k in (1, 3, 2):
            qy(h, k, 0).start()
        for d in range(2):
            pz(h, d, 1, 0, False).start()
        spread(h, 0, 0)
        for d in range(2):
            qz(h, d, 1, 0, 0, False).start()

    def join(h):
        for k in (1, 3, 2):
            qy(h, k, 1).wait_recv()
            for d in range(2):
                qz(h, d, 1, Y - k, 0, False).start()

    def step(h, s, first=False, last=False):
        for d in range(2):
            pz(h, d, s, 1, False).wait_recv()
            pz(h, d, s + 1, 0, last).start()
            spread(h, slot_of(d, s), -sign[d] * s)
        for n, e in enumerate(order):
            if n == 2:
                if first:
                    relay(h, 0, 0)
                else:
                    for d in range(2):
                        relay(h, slot_of(d, s - 1), -sign[d] * (s - 1))
            for d in range(2):
                qz(h, d, s, e, 1, False).wait_recv()
                qz(h, d, s + 1, e, 0, last).start()

    def steps(h, low, high):
        def body(s, carry):
            step(h, s)
            return carry

        lax.fori_loop(low, high, body, 0)

    def final(h):
        for d in range(2):
            pz(h, d, far, 1, True).wait_recv()
        spread(h, far, far)
        for d in range(2):
            relay(h, slot_of(d, far - 1), -sign[d] * (far - 1))

    def tail(h):
        for e in order:
            for d in range(2):
                qz(h, d, far, e, 1, True).wait_recv()
        relay(h, far, far)

        def rest(i, carry):
            dz = jnp.where(i <= far, -i, i - far)
            for kind in (2, 3):
                py(h, i, dz, kind, 1).wait_recv()
            return carry

        lax.fori_loop(0, nz, rest, 0)

    def b_copy(k, back):
        src = lax.rem(c - back * k + nc, nc)
        ref = B.at[pl.ds(pl.multiple_of(src * kc, kc), kc), :]
        return remote(ref, ref, b_s.at[k], b_r.at[k], at_c(k))

    def x_copy(h, k, back):
        to = lax.rem(c + (1 - back) * k, nc)
        src = lax.rem(c - back * k + nc, nc)
        return remote(
            L.at[pl.ds(h * oh, oh), pl.ds(pl.multiple_of(to * occ, occ), occ), :],
            R.at[src, pl.ds(h * oh, oh)],
            x_s.at[h, k], x_r.at[h, k], at_c(k),
        )

    def n_copy(buf, ss, rs, me, k, n, dev, back):
        ref = buf.at[lax.rem(me - back * k + n, n)]
        return remote(ref, ref, ss.at[k], rs.at[k], dev)

    def product(h, low, high):
        def body(i, carry):
            cols = pl.ds(pl.multiple_of(i * 2 * OCC, 2 * OCC), 2 * OCC)
            part = lax.dot_general(
                A[h, :, cols], B[...], (((0,), (0,)), ((), ())), preferred_element_type=jnp.float32
            )
            L[pl.ds(h * oh + 2 * i, 2)] = part.reshape(2, OCC, n_dev)
            return carry

        lax.fori_loop(low, high, body, 0)

    def exchange(h):
        for k in range(1, nc):
            x_copy(h, k, 0).start()
        own = pltpu.make_async_copy(
            L.at[pl.ds(h * oh, oh), pl.ds(pl.multiple_of(c * occ, occ), occ), :],
            R.at[c, pl.ds(h * oh, oh)],
            loc_sem.at[h],
        )
        own.start()
        own.wait()

    begin(0)
    for k in range(1, nc):
        b_copy(k, 0).start()
    join(0)
    step(0, 1, first=True)
    steps(0, 2, far - 2)
    begin(1)
    step(0, far - 2)
    join(1)
    step(0, far - 1, last=True)
    step(1, 1, first=True)
    final(0)
    step(1, 2)
    tail(0)
    for k in range(1, nc):
        b_copy(k, 1).wait_recv()
    product(0, 0, oh // 4)
    step(1, 3)
    product(0, oh // 4, oh // 2)
    exchange(0)
    steps(1, 4, far - 1)
    step(1, far - 1, last=True)
    final(1)
    tail(1)
    product(1, 0, oh // 2)
    exchange(1)

    for h in range(H):
        for k in range(1, nc):
            x_copy(h, k, 1).wait_recv()

        def add(src, carry):
            for o in range(0, oh, 8):
                got = jnp.swapaxes(R[src, pl.ds(h * oh + o, 8)], 0, 1)
                at = pl.ds(pl.multiple_of(src * occ + h * oh + o, 8), 8)
                s_ref[:, at, :] = L[:, at, :] + got
            return carry

        lax.fori_loop(0, nc, add, 0)

    def squares(i, carry):
        v = s_ref[i]
        v = v * v
        t = v[:, :TILE]
        for q in range(1, n_dev // TILE):
            t = t + v[:, q * TILE:(q + 1) * TILE]
        NZ[z, pl.ds(i, 1), :] = jnp.sum(t.T, axis=0, keepdims=True)
        return carry

    lax.fori_loop(0, occ, squares, 0)
    for k in range(1, nz):
        n_copy(NZ, nz_s, nz_r, z, k, nz, at_z(k), 0).start()
    for k in range(1, nz):
        n_copy(NZ, nz_s, nz_r, z, k, nz, at_z(k), 1).wait_recv()
    total = NZ[0]
    for q in range(1, nz):
        total = total + NZ[q]
    NY[y] = total
    for k in range(1, Y):
        n_copy(NY, ny_s, ny_r, y, k, Y, at_y(k), 0).start()
    for k in range(1, Y):
        n_copy(NY, ny_s, ny_r, y, k, Y, at_y(k), 1).wait_recv()
    total = NY[0]
    for q in range(1, Y):
        total = total + NY[q]
    n_ref[...] = jnp.sqrt(total / WIDTH + 1e-06)

    for h in range(H):
        for d in range(2):
            def sent(s, carry):
                pz(h, d, s, 0, False).wait_send()
                for e in range(Y):
                    qz(h, d, s, e, 0, False).wait_send()
                return carry

            lax.fori_loop(1, far, sent, 0)
            pz(h, d, far, 0, True).wait_send()
            for e in range(Y):
                qz(h, d, far, e, 0, True).wait_send()

        def sent_y(i, carry):
            dz = jnp.where(i <= far, -i, i - far)
            for kind in range(4):
                py(h, i, dz, kind, 0).wait_send()
            return carry

        lax.fori_loop(0, nz, sent_y, 0)
        for k in range(1, Y):
            qy(h, k, 0).wait_send()
        for k in range(1, nc):
            x_copy(h, k, 0).wait_send()
    for k in range(1, nc):
        b_copy(k, 0).wait_send()
    for k in range(1, nz):
        n_copy(NZ, nz_s, nz_r, z, k, nz, at_z(k), 0).wait_send()
    for k in range(1, Y):
        n_copy(NY, ny_s, ny_r, y, k, Y, at_y(k), 0).wait_send()


def local(nrow, nc, amplitudes, integrals, amp_mask, int_mask):
    kb, m_dev = amplitudes.shape
    kc, n_dev = integrals.shape
    nz = nrow // Y
    k_all = kb * nrow
    occ = m_dev // OCC
    far = nz // 2
    dma = pltpu.SemaphoreType.DMA
    pairs = [(H, 2, far + 1), (H, 2, far + 1, Y), (H, nz, 4), (H, Y), (nc,), (H, nc), (nz,), (Y,)]
    summed, norm = pl.pallas_call(
        functools.partial(kernel, nz, nc),
        out_shape=(
            jax.ShapeDtypeStruct((occ, OCC, n_dev), jnp.float32),
            jax.ShapeDtypeStruct((occ, OCC), jnp.float32),
        ),
        in_specs=[
            pl.BlockSpec(memory_space=pl.ANY),
        ] * 4,
        out_specs=(
            pl.BlockSpec(memory_space=pltpu.VMEM),
            pl.BlockSpec(memory_space=pltpu.VMEM),
        ),
        scratch_shapes=[
            pltpu.VMEM((H, k_all, m_dev // H), jnp.bfloat16),
            pltpu.VMEM((k_all, n_dev), jnp.bfloat16),
            pltpu.VMEM((occ, OCC, n_dev), jnp.float32),
            pltpu.VMEM((nc, occ, occ, n_dev), jnp.float32),
            pltpu.VMEM((nz, occ, OCC), jnp.float32),
            pltpu.VMEM((Y, occ, OCC), jnp.float32),
            pltpu.VMEM((kb, m_dev), jnp.bfloat16),
            pltpu.VMEM((kc, n_dev), jnp.bfloat16),
            pltpu.SMEM((8, amp_mask.shape[1]), jnp.int32),
            pltpu.SMEM((kc // kb, int_mask.shape[1]), jnp.int32),
            dma((4,)),
            dma((H,)),
        ] + [dma(p) for p in pairs for _ in range(2)],
        compiler_params=pltpu.CompilerParams(
            collective_id=0, has_side_effects=True, vmem_limit_bytes=60 << 20,
        ),
    )(amp_mask, int_mask, amplitudes, integrals)
    return summed.reshape(m_dev, n_dev) / norm.reshape(m_dev)[:, None], norm.reshape(m_dev)


def solution(mesh):
    return jax.shard_map(
        functools.partial(local, mesh.shape["row"], mesh.shape["col"]),
        mesh=mesh,
        in_specs=(P("row", "col"), P("col", "row"), P(), P()),
        out_specs=(P("col", "row"), P("col")),
        check_vma=False,
    )
```

```python
import functools

import jax
import jax.numpy as jnp
from jax import lax
from jax.experimental import pallas as pl
from jax.experimental.pallas import tpu as pltpu
from jax.sharding import PartitionSpec as P

TILE = 128
OCC = 128
Y = 4
H = 2
CUTS = ((0, 8), (8, 16))
PART = (5, 5)
MESH = pl.DeviceIdType.MESH
WIDTH = 16384


def kernel(
    nz, nc, am_ref, bm_ref, a_ref, b_ref, out_ref, n_ref,
    A, B, L, R, NZ, NY, s_ref, out_sem,
    a_own, b_own, am_own, bm_own, in_sem,
    loc_sem,
    pz_s, pz_r, qz_s, qz_r, py_s, py_r, qy_s, qy_r,
    b_s, b_r, x_s, x_r, nz_s, nz_r, ny_s, ny_r,
):
    kb, m_dev = a_ref.shape
    kc, n_dev = b_ref.shape
    half = kb // 2
    occ = m_dev // OCC
    start_of = [a * occ // 16 for a, b in CUTS]
    count_of = [(b - a) * occ // 16 for a, b in CUTS]
    low = [a * OCC for a in start_of]
    mid = [low[h] + PART[h] * m_dev // 16 for h in range(H)]
    high = [low[h] + count_of[h] * OCC for h in range(H)]
    far = nz // 2
    r = lax.axis_index("row")
    c = lax.axis_index("col")
    z = r // Y
    y = r % Y

    def at_z(d):
        return (lax.rem(z + d + 2 * nz, nz) * Y + y, c)

    def at_y(d):
        return (z * Y + lax.rem(y + d + 2 * Y, Y), c)

    def at_c(k):
        return (r, lax.rem(c + k, nc))

    def remote(src, dst, ss, rs, dev):
        return pltpu.make_async_remote_copy(
            src_ref=src, dst_ref=dst, send_sem=ss, recv_sem=rs,
            device_id=dev, device_id_type=MESH,
        )

    loads = (
        pltpu.make_async_copy(am_ref.at[pl.ds(pl.multiple_of(r // 8 * 8, 8), 8)], am_own, in_sem.at[0]),
        pltpu.make_async_copy(bm_ref.at[pl.ds(pl.multiple_of(c * (kc // kb), kc // kb), kc // kb)], bm_own, in_sem.at[1]),
        pltpu.make_async_copy(a_ref, a_own, in_sem.at[2]),
        pltpu.make_async_copy(b_ref, b_own, in_sem.at[3]),
    )
    for load in loads:
        load.start()

    barrier = pltpu.get_barrier_semaphore()
    for k in range(1, nz):
        pl.semaphore_signal(barrier, inc=1, device_id=at_z(k), device_id_type=MESH)
    for k in range(1, Y):
        pl.semaphore_signal(barrier, inc=1, device_id=at_y(k), device_id_type=MESH)
    for k in range(1, nc):
        pl.semaphore_signal(barrier, inc=1, device_id=at_c(k), device_id_type=MESH)

    for load in loads:
        load.wait()
    for t in range(m_dev // TILE):
        keep = am_own[r % 8, c * (m_dev // TILE) + t].astype(jnp.float32)
        lo = t * TILE
        val = (a_own[:, lo:lo + TILE].astype(jnp.float32) * keep).astype(jnp.bfloat16)
        A[pl.ds(pl.multiple_of(r * kb, kb), kb), lo:lo + TILE] = val
    for u in range(kc // kb):
        for t in range(n_dev // TILE):
            keep = bm_own[u, r * (n_dev // TILE) + t].astype(jnp.float32)
            val = b_own[u * kb:(u + 1) * kb, t * TILE:(t + 1) * TILE].astype(jnp.float32) * keep
            B[pl.ds(pl.multiple_of(c * kc + u * kb, kb), kb), t * TILE:(t + 1) * TILE] = val.astype(jnp.bfloat16)
    pl.semaphore_wait(barrier, nz - 1 + Y - 1 + nc - 1)

    def block(h, dz, dy, first, rows):
        zz = lax.rem(z + dz + 2 * nz, nz)
        yy = lax.rem(y + dy + 2 * Y, Y)
        return A.at[pl.ds(pl.multiple_of((zz * Y + yy) * kb + first, half), rows), low[h]:mid[h]]

    def rest_of(h, dz, dy, first, rows):
        zz = lax.rem(z + dz + 2 * nz, nz)
        yy = lax.rem(y + dy + 2 * Y, Y)
        return A.at[pl.ds(pl.multiple_of((zz * Y + yy) * kb + first, half), rows), mid[h]:high[h]]

    sign = (1, -1)

    def pz(h, d, s, back, last):
        ref = block(h, -sign[d] * (s - 1 + back), 0, d * half if last else 0, half if last else kb)
        return remote(ref, ref, pz_s.at[h, d, s], pz_r.at[h, d, s], at_z(sign[d]))

    def qz(h, d, s, e, back, last):
        ref = rest_of(h, -sign[d] * (s - 1 + back), e, d * half if last else 0, half if last else kb)
        return remote(ref, ref, qz_s.at[h, d, s, e], qz_r.at[h, d, s, e], at_z(sign[d]))

    def py(h, slot, dz, kind, back):
        d = kind % 2
        whole = kind < 2
        dy = -sign[d] * ((0 if whole else 1) + back)
        ref = block(h, dz, dy, 0 if whole else d * half, kb if whole else half)
        return remote(ref, ref, py_s.at[h, slot, kind], py_r.at[h, slot, kind], at_y(sign[d]))

    def qy(h, k, back):
        ref = rest_of(h, 0, -back * k, 0, kb)
        return remote(ref, ref, qy_s.at[h, k], qy_r.at[h, k], at_y(k))

    def slot_of(d, s):
        return s if d == 0 else far + s

    def spread(h, slot, dz):
        py(h, slot, dz, 0, 0).start()
        py(h, slot, dz, 1, 0).start()

    def relay(h, slot, dz):
        py(h, slot, dz, 0, 1).wait_recv()
        py(h, slot, dz, 2, 0).start()
        py(h, slot, dz, 1, 1).wait_recv()
        py(h, slot, dz, 3, 0).start()

    order = (0, 3, 1, 2)

    def begin(h):
        for k in (1, 3, 2):
            qy(h, k, 0).start()
        for d in range(2):
            pz(h, d, 1, 0, False).start()
        spread(h, 0, 0)
        for d in range(2):
            qz(h, d, 1, 0, 0, False).start()

    def join(h):
        for k in (1, 3, 2):
            qy(h, k, 1).wait_recv()
            for d in range(2):
                qz(h, d, 1, Y - k, 0, False).start()

    def step(h, s, first=False, last=False):
        for d in range(2):
            pz(h, d, s, 1, False).wait_recv()
            pz(h, d, s + 1, 0, last).start()
            spread(h, slot_of(d, s), -sign[d] * s)
        for n, e in enumerate(order):
            if n == 2:
                if first:
                    relay(h, 0, 0)
                else:
                    for d in range(2):
                        relay(h, slot_of(d, s - 1), -sign[d] * (s - 1))
            for d in range(2):
                qz(h, d, s, e, 1, False).wait_recv()
                qz(h, d, s + 1, e, 0, last).start()

    def steps(h, begin_at, end_at):
        def body(s, carry):
            step(h, s)
            return carry

        lax.fori_loop(begin_at, end_at, body, 0)

    def final(h):
        for d in range(2):
            pz(h, d, far, 1, True).wait_recv()
        spread(h, far, far)
        for d in range(2):
            relay(h, slot_of(d, far - 1), -sign[d] * (far - 1))

    def tail(h):
        for e in order:
            for d in range(2):
                qz(h, d, far, e, 1, True).wait_recv()
        relay(h, far, far)

        def rest(i, carry):
            dz = jnp.where(i <= far, -i, i - far)
            for kind in (2, 3):
                py(h, i, dz, kind, 1).wait_recv()
            return carry

        lax.fori_loop(0, nz, rest, 0)

    def b_copy(k, back):
        src = lax.rem(c - back * k + nc, nc)
        ref = B.at[pl.ds(pl.multiple_of(src * kc, kc), kc), :]
        return remote(ref, ref, b_s.at[k], b_r.at[k], at_c(k))

    def x_copy(h, k, back):
        to = lax.rem(c + (1 - back) * k, nc)
        src = lax.rem(c - back * k + nc, nc)
        return remote(
            L.at[pl.ds(start_of[h], count_of[h]), pl.ds(pl.multiple_of(to * occ, occ), occ), :],
            R.at[src, pl.ds(start_of[h], count_of[h])],
            x_s.at[h, k], x_r.at[h, k], at_c(k),
        )

    def n_copy(buf, ss, rs, me, k, n, dev, back):
        ref = buf.at[lax.rem(me - back * k + n, n)]
        return remote(ref, ref, ss.at[k], rs.at[k], dev)

    def product(h, begin_at, end_at):
        def body(i, carry):
            cols = pl.ds(pl.multiple_of(low[h] + i * 2 * OCC, 2 * OCC), 2 * OCC)
            part = lax.dot_general(
                A[:, cols], B[...], (((0,), (0,)), ((), ())), preferred_element_type=jnp.float32
            )
            L[pl.ds(start_of[h] + 2 * i, 2)] = part.reshape(2, OCC, n_dev)
            return carry

        lax.fori_loop(begin_at, end_at, body, 0)

    def exchange(h):
        for k in range(1, nc):
            x_copy(h, k, 0).start()
        own = pltpu.make_async_copy(
            L.at[pl.ds(start_of[h], count_of[h]), pl.ds(pl.multiple_of(c * occ, occ), occ), :],
            R.at[c, pl.ds(start_of[h], count_of[h])],
            loc_sem.at[h],
        )
        own.start()
        own.wait()

    begin(0)
    for k in range(1, nc):
        b_copy(k, 0).start()
    join(0)
    step(0, 1, first=True)
    steps(0, 2, 4)
    begin(1)
    step(0, 4)
    join(1)
    step(0, 5)
    step(1, 1, first=True)
    step(0, 6)
    step(1, 2)
    step(0, far - 1, last=True)
    step(1, 3)
    final(0)
    step(1, 4)
    tail(0)
    for k in range(1, nc):
        b_copy(k, 1).wait_recv()
    product(0, 0, count_of[0] // 4)
    step(1, 5)
    product(0, count_of[0] // 4, count_of[0] // 2)
    exchange(0)
    steps(1, 6, far - 1)
    step(1, far - 1, last=True)
    final(1)
    tail(1)
    product(1, 0, count_of[1] // 2)
    exchange(1)

    done = 0
    for h in range(H):
        for k in range(1, nc):
            x_copy(h, k, 1).wait_recv()
        ready = (start_of[h] + count_of[h]) // 8 * 8

        def add(src, carry):
            for o in range(done, ready, 8):
                got = jnp.swapaxes(R[src, pl.ds(o, 8)], 0, 1)
                at = pl.ds(pl.multiple_of(src * occ + o, 8), 8)
                s_ref[:, at, :] = L[:, at, :] + got
            return carry

        lax.fori_loop(0, nc, add, 0)
        done = ready

    out = pltpu.make_async_copy(s_ref, out_ref, out_sem)
    out.start()

    def squares(i, carry):
        v = s_ref[i]
        v = v * v
        t = v[:, :TILE]
        for q in range(1, n_dev // TILE):
            t = t + v[:, q * TILE:(q + 1) * TILE]
        NZ[z, pl.ds(i, 1), :] = jnp.sum(t.T, axis=0, keepdims=True)
        return carry

    lax.fori_loop(0, occ, squares, 0)
    for k in range(1, nz):
        n_copy(NZ, nz_s, nz_r, z, k, nz, at_z(k), 0).start()

    for h in range(H):
        for d in range(2):
            def sent(s, carry):
                pz(h, d, s, 0, False).wait_send()
                for e in range(Y):
                    qz(h, d, s, e, 0, False).wait_send()
                return carry

            lax.fori_loop(1, far, sent, 0)
            pz(h, d, far, 0, True).wait_send()
            for e in range(Y):
                qz(h, d, far, e, 0, True).wait_send()

        def sent_y(i, carry):
            dz = jnp.where(i <= far, -i, i - far)
            for kind in range(4):
                py(h, i, dz, kind, 0).wait_send()
            return carry

        lax.fori_loop(0, nz, sent_y, 0)
        for k in range(1, Y):
            qy(h, k, 0).wait_send()
        for k in range(1, nc):
            x_copy(h, k, 0).wait_send()
    for k in range(1, nc):
        b_copy(k, 0).wait_send()

    for k in range(1, nz):
        n_copy(NZ, nz_s, nz_r, z, k, nz, at_z(k), 1).wait_recv()
    total = NZ[0]
    for q in range(1, nz):
        total = total + NZ[q]
    NY[y] = total
    for k in range(1, Y):
        n_copy(NY, ny_s, ny_r, y, k, Y, at_y(k), 0).start()
    for k in range(1, Y):
        n_copy(NY, ny_s, ny_r, y, k, Y, at_y(k), 1).wait_recv()
    total = NY[0]
    for q in range(1, Y):
        total = total + NY[q]
    n_ref[...] = jnp.sqrt(total / WIDTH + 1e-06)
    for k in range(1, nz):
        n_copy(NZ, nz_s, nz_r, z, k, nz, at_z(k), 0).wait_send()
    for k in range(1, Y):
        n_copy(NY, ny_s, ny_r, y, k, Y, at_y(k), 0).wait_send()
    out.wait()


def local(nrow, nc, amplitudes, integrals, amp_mask, int_mask):
    kb, m_dev = amplitudes.shape
    kc, n_dev = integrals.shape
    nz = nrow // Y
    k_all = kb * nrow
    occ = m_dev // OCC
    far = nz // 2
    dma = pltpu.SemaphoreType.DMA
    pairs = [(H, 2, far + 1), (H, 2, far + 1, Y), (H, nz, 4), (H, Y), (nc,), (H, nc), (nz,), (Y,)]
    summed, norm = pl.pallas_call(
        functools.partial(kernel, nz, nc),
        out_shape=(
            jax.ShapeDtypeStruct((occ, OCC, n_dev), jnp.float32),
            jax.ShapeDtypeStruct((occ, OCC), jnp.float32),
        ),
        in_specs=[
            pl.BlockSpec(memory_space=pl.ANY),
        ] * 4,
        out_specs=(
            pl.BlockSpec(memory_space=pl.ANY),
            pl.BlockSpec(memory_space=pltpu.VMEM),
        ),
        scratch_shapes=[
            pltpu.VMEM((k_all, m_dev), jnp.bfloat16),
            pltpu.VMEM((k_all, n_dev), jnp.bfloat16),
            pltpu.VMEM((occ, OCC, n_dev), jnp.float32),
            pltpu.VMEM((nc, occ, occ, n_dev), jnp.float32),
            pltpu.VMEM((nz, occ, OCC), jnp.float32),
            pltpu.VMEM((Y, occ, OCC), jnp.float32),
            pltpu.VMEM((occ, OCC, n_dev), jnp.float32),
            dma,
            pltpu.VMEM((kb, m_dev), jnp.bfloat16),
            pltpu.VMEM((kc, n_dev), jnp.bfloat16),
            pltpu.SMEM((8, amp_mask.shape[1]), jnp.int32),
            pltpu.SMEM((kc // kb, int_mask.shape[1]), jnp.int32),
            dma((4,)),
            dma((H,)),
        ] + [dma(p) for p in pairs for _ in range(2)],
        compiler_params=pltpu.CompilerParams(
            collective_id=0, has_side_effects=True, vmem_limit_bytes=60 << 20,
        ),
    )(amp_mask, int_mask, amplitudes, integrals)
    return summed.reshape(m_dev, n_dev) / norm.reshape(m_dev)[:, None], norm.reshape(m_dev)


def solution(mesh):
    return jax.shard_map(
        functools.partial(local, mesh.shape["row"], mesh.shape["col"]),
        mesh=mesh,
        in_specs=(P("row", "col"), P("col", "row"), P(), P()),
        out_specs=(P("col", "row"), P("col")),
        check_vma=False,
    )
```
